32 devices in a mesh: table: 8 (over z, core), bal: 4 (over y, x).
Axes of the slice: x: 2, y: 2, z: 4, core: 2. Of those that a mesh axis runs over, the one named last changes fastest.
Arguments:
- item_ids: int32 [8192], P(('table', 'bal')), may hold values from 0 to 8191, as said below
- hot_slot: int32 [8192], replicated, may hold values from 0 to 1024, as said below
- hot_rows: bfloat16 [1024, 512], replicated, may hold values from -6 to 6
- cold_rows: bfloat16 [8192, 512], P('table'), may hold values from -6 to 6
- hist_lengths: int32 [64], replicated, may hold values from 1 to 128
- out_grad: bfloat16 [8192, 512], P(('table', 'bal')), may hold values from -6 to 6
- w_uvqk: bfloat16 [512, 2048], replicated, may hold values from -0.25 to 0.25
- w_out: bfloat16 [512, 512], replicated, may hold values from -0.25 to 0.25
Outputs:
- layer_out: bfloat16 [8192, 512], P(('table', 'bal'))
- grad_uvqk: float32 [4096, 2048], P(('table', 'bal'))
- grad_out_proj: float32 [4096, 512], P(('table', 'bal'))
The draws below stay inside these ranges and needn't reach their ends.
Inputs may be any that keep to these rules, and one draw needn't show every extreme that they name: `item_ids`: item i lies in table shard i // 1024. In each device's block of 256 token slots at most 32 tokens with cold items name items of one shard, and some shard gets exactly 32 of them in every block. `hot_slot`: each value below 1024 is taken by exactly one item; 1024 marks a cold item.
All inputs are finite; a program needn't handle non-finite values.
Results may differ from the reference program's by a relative error of at most 0.012.
Values may be sent and summed in bfloat16 or wider, within the bound.
No kernel may reach another device: no remote copies, remote signals or barrier semaphores. Data moves between devices by JAX's collectives and lax.ppermute only.
A program may use at most 64 MiB of HBM per device.

```python
import math
import jax
import jax.numpy as jnp
from jax import lax

D = 512
HEADS = 4
MAXLEN = 128
USR_DEV = 2
ROWS_DEV = 1024
HOT = 1024
TOK_DEV = 256
USERS = 64
TOKENS = 8192
ITEMS = 8192
N_TABLE = 8
N_BAL = 4


def hot_list(key):
    half_rows = ROWS_DEV // 2
    owner_count = ITEMS // ROWS_DEV
    chosen = jax.random.permutation(jax.random.fold_in(key, 7), owner_count * half_rows)[:HOT]
    return (chosen // half_rows * ROWS_DEV + chosen % half_rows).astype(jnp.int32)


def draw_hot_slot(key, part):
    hot_items = hot_list(key)
    return jnp.full((ITEMS,), HOT, jnp.int32).at[hot_items].set(jnp.arange(HOT, dtype=jnp.int32))


def draw_item_ids(key, part):
    half_rows = ROWS_DEV // 2
    owner_count = ITEMS // ROWS_DEV
    block_count = TOKENS // TOK_DEV
    hot_items = hot_list(key)
    key_perm, key_forced, key_coin, key_hot, key_cold = jax.random.split(jax.random.fold_in(key, 11), 5)
    shuffles = jax.vmap(lambda one_key: jax.random.permutation(one_key, TOK_DEV))(jax.random.split(key_perm, block_count))
    owner_of = (shuffles % owner_count).astype(jnp.int32)
    forced_owner = jax.random.randint(key_forced, (block_count, 1), 0, owner_count)
    coin_flip = jax.random.randint(key_coin, (block_count, TOK_DEV), 0, 2)
    use_hot = (coin_flip == 1) & (owner_of != forced_owner)
    hot_pick = hot_items[jax.random.randint(key_hot, (block_count, TOK_DEV), 0, HOT)]
    cold_pick = owner_of * ROWS_DEV + half_rows + jax.random.randint(key_cold, (block_count, TOK_DEV), 0, ROWS_DEV - half_rows)
    return jnp.where(use_hot, hot_pick, cold_pick).astype(jnp.int32).reshape(TOKENS)


def plant(values, rng, least, high):
    spot = [jax.random.randint(jax.random.fold_in(rng, axis), (), 0, length) for axis, length in enumerate(values.shape)]
    widest = values.shape.index(max(values.shape))
    beside = spot[:widest] + [(spot[widest] + 1) % values.shape[widest]] + spot[widest + 1:]
    return values.at[tuple(spot)].set(least).at[tuple(beside)].set(high)


def level_of(stream_key, extent, cuts, low, high):
    def one(dim, shards_of):
        heights = jax.random.uniform(jax.random.fold_in(jax.random.fold_in(stream_key, 6), dim), (shards_of,), jnp.float32, low / len(cuts), high / len(cuts))
        return jnp.repeat(jnp.exp(heights), extent[dim] // shards_of).reshape((-1,) + (1,) * (len(extent) - dim - 1))

    gain = one(*cuts[0])
    for cut in cuts[1:]:
        gain = gain * one(*cut)
    return gain


def normal_values(key, dims, width, most, shards=(), kind=jnp.bfloat16):
    gain = level_of(key, dims, shards, -0.22, 0.18) if shards else 1.0
    result = jax.random.normal(key, dims, jnp.float32) * width * gain
    return jnp.minimum(jnp.maximum(result, -most), most).astype(kind)


def setup_inputs(seed: int = 0) -> dict:
    keys = jax.random.split(jax.random.key(seed), 9)
    return {
        "item_ids": draw_item_ids(jax.random.fold_in(keys[8], 71), 0),
        "hot_slot": draw_hot_slot(jax.random.fold_in(keys[8], 71), 0),
        "hot_rows": normal_values(keys[2], (HOT, D), 1.0, 6.0),
        "cold_rows": normal_values(keys[3], (ITEMS, D), 1.0, 6.0, ((0, 8),)),
        "hist_lengths": plant(jax.random.randint(keys[4], (USERS,), 1, MAXLEN + 1), jax.random.fold_in(keys[4], 1), 1, MAXLEN).astype(jnp.int32),
        "out_grad": normal_values(keys[5], (TOKENS, D), 1.0, 6.0, ((0, 32),)),
        "w_uvqk": normal_values(keys[6], (D, 4 * D), D ** -0.5, 0.25),
        "w_out": normal_values(keys[7], (D, D), D ** -0.5, 0.25),
    }


def norm_rows(values_in):
    average = lax.optimization_barrier(jnp.mean(values_in, axis=-1, keepdims=True))
    centred = values_in - average
    spread = lax.optimization_barrier(jnp.mean(centred * centred, axis=-1, keepdims=True))
    return centred * lax.rsqrt(spread + 1e-05)

def attend(hidden, length):
    row_count = hidden.shape[0]
    features = hidden.shape[1] // 4
    head_size = features // HEADS
    activated = jax.nn.silu(hidden)
    gate_part = activated[:, :features].astype(jnp.bfloat16)
    value_part = activated[:, features:2 * features].astype(jnp.bfloat16)
    query_part = activated[:, 2 * features:3 * features].astype(jnp.bfloat16)
    key_part = activated[:, 3 * features:].astype(jnp.bfloat16)
    query_heads = query_part.reshape(row_count, HEADS, head_size).astype(jnp.float32)
    key_heads = key_part.reshape(row_count, HEADS, head_size).astype(jnp.float32)
    value_heads = value_part.reshape(row_count, HEADS, head_size).astype(jnp.float32)
    scores = jnp.einsum('ihe,jhe->hij', query_heads, key_heads) * (1.0 / math.sqrt(head_size))
    position = jnp.arange(row_count, dtype=jnp.int32)
    allowed = (position[None, :] <= position[:, None]) & (position[:, None] < length)
    weights = jnp.where(allowed[None], jax.nn.silu(scores), 0.0).astype(jnp.bfloat16)
    mixed = jnp.einsum('hij,jhe->ihe', weights.astype(jnp.float32), value_heads).reshape(row_count, features)
    return (norm_rows(mixed) * gate_part.astype(jnp.float32)).astype(jnp.bfloat16)

def user_pass(user_emb, user_cot, length, w_uvqk, w_out, grad_scale):
    row_count = user_emb.shape[0]
    normed = norm_rows(user_emb.astype(jnp.float32)).astype(jnp.bfloat16)
    hidden = jnp.dot(normed, w_uvqk, preferred_element_type=jnp.float32)
    gated, pullback = jax.vjp(lambda hidden_in: attend(hidden_in, length), hidden)
    output = (user_emb.astype(jnp.float32) + jnp.dot(gated, w_out, preferred_element_type=jnp.float32)).astype(jnp.bfloat16)
    is_valid = jnp.arange(row_count, dtype=jnp.int32) < length
    signal = (jnp.where(is_valid[:, None], user_cot.astype(jnp.float32), 0.0) * grad_scale).astype(jnp.bfloat16)
    back_signal = jnp.dot(signal, w_out.T, preferred_element_type=jnp.float32).astype(jnp.bfloat16)
    grad_hidden = pullback(back_signal)[0].astype(jnp.bfloat16)
    grad_first = jnp.einsum('td,tf->df', normed.astype(jnp.float32), grad_hidden.astype(jnp.float32))
    grad_second = jnp.einsum('td,tf->df', gated.astype(jnp.float32), signal.astype(jnp.float32))
    return (output, grad_first, grad_second)

def reference(item_ids, hot_slot, hot_rows, cold_rows, hist_lengths, out_grad, w_uvqk, w_out):
    hot_index = hot_slot[item_ids]
    is_hot = hot_index < HOT
    embedded = jnp.where(is_hot[:, None], hot_rows[jnp.minimum(hot_index, HOT - 1)], cold_rows[item_ids])
    group_users = N_BAL * USR_DEV
    grad_scale = 1.0 / math.sqrt(N_BAL * USR_DEV * MAXLEN)
    grouped = embedded.reshape(N_TABLE, group_users, MAXLEN, D)
    cotangent = out_grad.reshape(N_TABLE, group_users, MAXLEN, D)
    lengths = hist_lengths.reshape(N_TABLE, group_users)

    def per_group(inputs):

        def per_user(running, pieces):
            output, grad_first, grad_second = user_pass(pieces[0], pieces[1], pieces[2], w_uvqk, w_out, grad_scale)
            return ((running[0] + grad_first, running[1] + grad_second), output)
        initial = (jnp.zeros((D, 4 * D), jnp.float32), jnp.zeros((D, D), jnp.float32))
        totals, outputs = lax.scan(per_user, initial, inputs)
        return (outputs, totals[0], totals[1])
    outputs, grad_first, grad_second = lax.map(per_group, (grouped, cotangent, lengths))
    return (outputs.reshape(TOKENS, D), grad_first.reshape(N_TABLE * D, 4 * D), grad_second.reshape(N_TABLE * D, D))
```

```python
import functools
import math

import jax
import jax.numpy as jnp
from jax import lax
from jax.experimental import pallas as pl
from jax.experimental.pallas import tpu as pltpu
from jax.sharding import PartitionSpec as P

HEADS = 4
MAXLEN = 128
LANES = 128
F32 = jnp.float32
BF16 = jnp.bfloat16


def dot_nn(a, b):
    return lax.dot_general(a, b, (((1,), (0,)), ((), ())), preferred_element_type=F32)


def dot_nt(a, b):
    return lax.dot_general(a, b, (((1,), (1,)), ((), ())), preferred_element_type=F32)


def dot_tn(a, b):
    return lax.dot_general(a, b, (((0,), (0,)), ((), ())), preferred_element_type=F32)


def iota(shape, dim):
    return lax.broadcasted_iota(jnp.int32, shape, dim)


def sigmoid(x):
    return 0.5 + 0.5 * jnp.tanh(0.5 * x)


def norm_rows(x):
    centred = x - jnp.mean(x, axis=-1, keepdims=True)
    return centred * lax.rsqrt(jnp.mean(centred * centred, axis=-1, keepdims=True) + 1e-05)


def before_matrix(count):
    return (iota((count, count), 0) < iota((count, count), 1)).astype(BF16)


def table_lookup(table, ids):
    tokens = ids.shape[1]
    high = (iota((table.shape[0], tokens), 0) == ids // LANES).astype(BF16)
    lines = dot_tn(table, high)
    return jnp.sum(jnp.where(iota(lines.shape, 0) == ids % LANES, lines, 0.0), axis=0, keepdims=True)


def serve_kernel(hot_count, ids_ref, hot_ref, cold_ref, out_ref):
    sources, _, tokens = ids_ref.shape
    shard_rows = cold_ref.shape[0]
    capacity = out_ref.shape[0] // sources
    first = lax.axis_index("table") * shard_rows
    cold_table = (hot_ref[...] >= hot_count).astype(F32).astype(BF16)
    before = before_matrix(tokens)
    group = math.gcd(sources, 8)

    def serve(start):
        local, marks = [], []
        for s in range(group):
            ids = ids_ref[start + s]
            row = ids - first
            mine = (row >= 0) & (row < shard_rows)
            marks.append(jnp.where(mine, table_lookup(cold_table, ids), 0.0))
            local.append(row.astype(F32))
        mark = jnp.concatenate(marks, axis=0)
        rank = dot_nn(mark.astype(BF16), before)
        picks = []
        for s in range(group):
            chosen = (iota((capacity, tokens), 0).astype(F32) == rank[s : s + 1]) & (marks[s] > 0.5)
            wanted = jnp.sum(jnp.where(chosen, local[s], 0.0), axis=1, keepdims=True)
            picks.append((iota((capacity, shard_rows), 1).astype(F32) == wanted).astype(F32))
        pick = jnp.concatenate(picks, axis=0).astype(BF16)
        return dot_nn(pick, cold_ref[...]).astype(BF16)

    if sources == group:
        out_ref[...] = serve(0)
    else:
        span = group * capacity

        def step(i, carry):
            out_ref[pl.ds(pl.multiple_of(i * span, span), span), :] = serve(i * group)
            return carry

        lax.fori_loop(0, sources // group, step, 0)


def own_kernel(shard_rows, scale, len_ref, ids_ref, hot_ref, hot_rows_ref, cot_ref, w_out_ref,
               emb_ref, pick_ref, signal_ref, back_ref):
    tokens = ids_ref.shape[1]
    hot_count = hot_rows_ref.shape[0]
    sources = lax.axis_size("table")
    capacity = tokens // sources
    ids = ids_ref[...]
    table = hot_ref[...]
    high = table_lookup((table // 256).astype(F32).astype(BF16), ids)
    low = table_lookup((table % 256).astype(F32).astype(BF16), ids)
    hot_index = high * 256.0 + low
    cold = hot_index >= hot_count
    row = ids - iota((sources, tokens), 0) * shard_rows
    mark = jnp.where((row >= 0) & (row < shard_rows) & cold, 1.0, 0.0)
    rank = dot_nn(mark.astype(BF16), before_matrix(tokens))
    place = rank + (iota((sources, tokens), 0) * capacity).astype(F32)
    slot = jnp.sum(mark * place, axis=0, keepdims=True) - jnp.where(cold, 0.0, 1.0)
    stacked = jnp.concatenate([slot, hot_index, jnp.zeros((6, tokens), F32)], axis=0)
    columns = jnp.transpose(stacked)
    pick_ref[...] = (
        (iota((tokens, tokens), 1).astype(F32) == columns[:, 0:1]).astype(F32).astype(BF16)
    )
    hot_pick = (iota((tokens, hot_count), 1).astype(F32) == columns[:, 1:2]).astype(F32).astype(BF16)
    emb_ref[...] = dot_nn(hot_pick, hot_rows_ref[...]).astype(BF16)
    users = tokens // MAXLEN
    first_user = (lax.axis_index("table") * lax.axis_size("bal") + lax.axis_index("bal")) * users
    for u in range(users):
        rows = slice(u * MAXLEN, (u + 1) * MAXLEN)
        valid = iota((MAXLEN, 1), 0) < len_ref[first_user + u]
        signal_ref[rows, :] = (jnp.where(valid, cot_ref[rows, :].astype(F32), 0.0) * scale).astype(BF16)
    back_ref[...] = dot_nt(signal_ref[...], w_out_ref[...]).astype(BF16)


def layer_kernel(len_ref, emb_ref, pick_ref, replies_ref, signal_ref, back_ref, w_ref, w_out_ref,
                 out_ref, *rest):
    pieces = rest[:4]
    normed_t, gated_t, grad, gated, slope = rest[4:]
    tokens, features = emb_ref.shape
    head = features // HEADS
    users = tokens // MAXLEN
    bal = lax.axis_size("bal")
    me = lax.axis_index("bal")
    first_user = (lax.axis_index("table") * bal + me) * users
    inv = 1.0 / math.sqrt(head)

    emb = dot_nn(pick_ref[...], replies_ref[...]) + emb_ref[...].astype(F32)
    normed = norm_rows(emb)
    normed_t[...] = jnp.transpose(normed).astype(BF16)
    normed = normed.astype(BF16)

    def part(index):
        hidden = dot_nn(normed, w_ref[:, index * features : (index + 1) * features])
        gate = sigmoid(hidden)
        act = hidden * gate
        slope[:, index * features : (index + 1) * features] = gate * (1.0 + hidden - act)
        return act.astype(BF16)

    gate_part, value_part, query_part, key_part = (part(i) for i in range(4))
    for u in range(users):
        rows = slice(u * MAXLEN, (u + 1) * MAXLEN)
        length = len_ref[first_user + u]
        at = iota((MAXLEN, MAXLEN), 0)
        allowed = (iota((MAXLEN, MAXLEN), 1) <= at) & (at < length)
        weights, slopes, mixes = [], [], []
        for h in range(HEADS):
            cols = slice(h * head, (h + 1) * head)
            score = dot_nt(query_part[rows, cols], key_part[rows, cols]) * inv
            s = sigmoid(score)
            a = score * s
            weight = jnp.where(allowed, a, 0.0).astype(BF16)
            weights.append(weight)
            slopes.append(jnp.where(allowed, s * (1.0 + score - a) * inv, 0.0))
            mixes.append(dot_nn(weight, value_part[rows, cols]))
        mixed = jnp.concatenate(mixes, axis=1)
        centred = mixed - jnp.mean(mixed, axis=-1, keepdims=True)
        rstd = lax.rsqrt(jnp.mean(centred * centred, axis=-1, keepdims=True) + 1e-05)
        unit = centred * rstd
        gate = gate_part[rows].astype(F32)
        gated[rows, :] = (unit * gate).astype(BF16)
        back = back_ref[rows, :].astype(F32)
        d_gate = (back * unit).astype(BF16).astype(F32)
        grad[rows, 0:features] = (d_gate * slope[rows, 0:features]).astype(BF16)
        d_unit = back * gate
        d_mixed = rstd * (
            d_unit
            - jnp.mean(d_unit, axis=-1, keepdims=True)
            - unit * jnp.mean(d_unit * unit, axis=-1, keepdims=True)
        )
        d_mixed = d_mixed.astype(BF16)
        for h in range(HEADS):
            cols = slice(h * head, (h + 1) * head)
            d_mix = d_mixed[:, cols]
            d_weight = dot_nt(d_mix, value_part[rows, cols]).astype(BF16).astype(F32)
            d_score = (d_weight * slopes[h]).astype(BF16)
            d_value = dot_tn(weights[h], d_mix)
            d_query = dot_nn(d_score, key_part[rows, cols])
            d_key = dot_tn(d_score, query_part[rows, cols])
            for index, value in ((1, d_value), (2, d_query), (3, d_key)):
                where = slice(index * features + h * head, index * features + (h + 1) * head)
                grad[rows, where] = (value.astype(BF16).astype(F32) * slope[rows, where]).astype(BF16)
    out_ref[...] = (emb + dot_nn(gated[...], w_out_ref[...])).astype(BF16)
    gated_t[...] = jnp.transpose(gated[...].astype(F32)).astype(BF16)

    block = features // bal
    width = pieces[0].shape[-1]
    total = grad.shape[1]
    low, high = bal // 2, 1
    for r in range(bal):
        start = pl.multiple_of((r ^ me) * block, block)
        left = normed_t[pl.ds(start, block), :]
        first_order, second_order = split_index(r, bal)
        target, index = (pieces[0], pieces[1])[first_order[0]], first_order[1]
        target[index] = dot_nn(left, grad[:, 0:width]).astype(BF16)
        target, index = (pieces[2], pieces[3])[second_order[0]], second_order[1]
        target[index, :, 0 : total - width] = dot_nn(left, grad[:, width:total]).astype(BF16)
        out_left = gated_t[pl.ds(start, block), :]
        target[index, :, total - width : width] = dot_nn(out_left, signal_ref[...]).astype(BF16)


def bit_orders(count):
    bits = [1 << k for k in range(count.bit_length() - 1)]
    half = len(bits) // 2
    return bits, bits[half:] + bits[:half]


def split_index(r, count):
    answers = []
    for order in bit_orders(count):
        bit = order[0]
        same = [k for k in range(count) if (k & bit) == (r & bit)]
        answers.append((0 if r & bit else 1, same.index(r)))
    return answers


def halve(send, keep, order, count):
    members = [k for k in range(count) if not k & order[0]]
    for step, bit in enumerate(order):
        got = lax.ppermute(send, "bal", [(i, i ^ bit) for i in range(count)])
        total = got.astype(F32) + keep.astype(F32)
        if step + 1 == len(order):
            return total[0]
        following = order[step + 1]
        pick = lambda on: [i for i, k in enumerate(members) if bool(k & following) == on]
        send = jnp.stack([total[i] for i in pick(True)]).astype(BF16)
        keep = jnp.stack([total[i] for i in pick(False)])
        members = [k for k in members if not k & following]


def per_device(item_ids, hot_slot, hot_rows, cold_rows, hist_lengths, out_grad, w_uvqk, w_out):
    owners = lax.axis_size("table")
    bal = lax.axis_size("bal")
    tokens = item_ids.shape[0]
    features = hot_rows.shape[1]
    hot_count = hot_rows.shape[0]
    shard_rows = cold_rows.shape[0]
    hidden = w_uvqk.shape[1]
    vmem = pl.BlockSpec(memory_space=pltpu.VMEM)
    smem = pl.BlockSpec(memory_space=pltpu.SMEM)
    hot_table = hot_slot.reshape(-1, LANES)

    everyone = jnp.broadcast_to(item_ids.reshape(1, 1, tokens), (owners, 1, tokens))
    asked = lax.all_to_all(everyone, "table", split_axis=0, concat_axis=0, tiled=True)
    found = pl.pallas_call(
        functools.partial(serve_kernel, hot_count),
        out_shape=jax.ShapeDtypeStruct((tokens, features), BF16),
        in_specs=[vmem] * 3,
        out_specs=vmem,
        name="serve",
    )(asked, hot_table, cold_rows)
    replies = lax.all_to_all(found, "table", split_axis=0, concat_axis=0, tiled=True)

    wide = jax.ShapeDtypeStruct((tokens, features), BF16)
    hot_emb, pick, signal, back = pl.pallas_call(
        functools.partial(own_kernel, shard_rows, 1.0 / math.sqrt(bal * tokens)),
        out_shape=(wide, jax.ShapeDtypeStruct((tokens, tokens), BF16), wide, wide),
        in_specs=[smem] + [vmem] * 5,
        out_specs=(vmem,) * 4,
        name="own",
    )(hist_lengths, item_ids.reshape(1, tokens), hot_table, hot_rows, out_grad, w_out)

    width = (hidden + features) // 2
    piece = jax.ShapeDtypeStruct((bal // 2, features // bal, width), BF16)
    layer_out, a_send, a_keep, b_send, b_keep = pl.pallas_call(
        layer_kernel,
        out_shape=(wide,) + (piece,) * 4,
        in_specs=[smem] + [vmem] * 7,
        out_specs=(vmem,) * 5,
        scratch_shapes=[
            pltpu.VMEM((features, tokens), BF16),
            pltpu.VMEM((features, tokens), BF16),
            pltpu.VMEM((tokens, hidden), BF16),
            pltpu.VMEM((tokens, features), BF16),
            pltpu.VMEM((tokens, hidden), F32),
        ],
        name="layer",
    )(hist_lengths, hot_emb, pick, replies, signal, back, w_uvqk, w_out)

    first_order, second_order = bit_orders(bal)
    a = halve(a_send, a_keep, first_order, bal)
    b = halve(b_send, b_keep, second_order, bal)
    grad_first = jnp.concatenate([a, b[:, : hidden - width]], axis=1)
    return (layer_out, grad_first, b[:, hidden - width :])


def solution(mesh):
    return jax.shard_map(
        per_device,
        mesh=mesh,
        in_specs=(
            P(("table", "bal")),
            P(),
            P(),
            P("table", None),
            P(),
            P(("table", "bal"), None),
            P(),
            P(),
        ),
        out_specs=(P(("table", "bal"), None), P(("table", "bal"), None), P(("table", "bal"), None)),
        check_vma=False,
    )
```

```python
import functools
import math

import jax
import jax.numpy as jnp
from jax import lax
from jax.experimental import pallas as pl
from jax.experimental.pallas import tpu as pltpu
from jax.sharding import PartitionSpec as P

HEADS = 4
MAXLEN = 128
LANES = 128
VM_SERVE = 8 << 20
VM_OWN = 8 << 20
VM_LAYER = 20 << 20
F32 = jnp.float32
BF16 = jnp.bfloat16


def dot_nn(a, b):
    return lax.dot_general(a, b, (((1,), (0,)), ((), ())), preferred_element_type=F32)


def dot_nt(a, b):
    return lax.dot_general(a, b, (((1,), (1,)), ((), ())), preferred_element_type=F32)


def dot_tn(a, b):
    return lax.dot_general(a, b, (((0,), (0,)), ((), ())), preferred_element_type=F32)


def iota(shape, dim):
    return lax.broadcasted_iota(jnp.int32, shape, dim)


def sigmoid(x):
    return 0.5 + 0.5 * jnp.tanh(0.5 * x)


def norm_rows(x):
    centred = x - jnp.mean(x, axis=-1, keepdims=True)
    return centred * lax.rsqrt(jnp.mean(centred * centred, axis=-1, keepdims=True) + 1e-05)


def before_matrix(count):
    return (iota((count, count), 0) < iota((count, count), 1)).astype(BF16)


def table_lookup(table, ids):
    tokens = ids.shape[1]
    high = (iota((table.shape[0], tokens), 0) == ids // LANES).astype(BF16)
    lines = dot_tn(table, high)
    return jnp.sum(jnp.where(iota(lines.shape, 0) == ids % LANES, lines, 0.0), axis=0, keepdims=True)


def serve_kernel(hot_count, ids_ref, hot_ref, cold_ref, out_ref):
    sources, _, tokens = ids_ref.shape
    shard_rows = cold_ref.shape[0]
    capacity = out_ref.shape[0] // sources
    first = lax.axis_index("table") * shard_rows
    cold_table = (hot_ref[...] >= hot_count).astype(F32).astype(BF16)
    before = before_matrix(tokens)
    group = math.gcd(sources, 8)

    def serve(start):
        local, marks = [], []
        for s in range(group):
            ids = ids_ref[start + s]
            row = ids - first
            mine = (row >= 0) & (row < shard_rows)
            marks.append(jnp.where(mine, table_lookup(cold_table, ids), 0.0))
            local.append(row.astype(F32))
        mark = jnp.concatenate(marks, axis=0)
        rank = dot_nn(mark.astype(BF16), before)
        picks = []
        for s in range(group):
            chosen = (iota((capacity, tokens), 0).astype(F32) == rank[s : s + 1]) & (marks[s] > 0.5)
            wanted = jnp.sum(jnp.where(chosen, local[s], 0.0), axis=1, keepdims=True)
            picks.append((iota((capacity, shard_rows), 1).astype(F32) == wanted).astype(F32))
        pick = jnp.concatenate(picks, axis=0).astype(BF16)
        return dot_nn(pick, cold_ref[...]).astype(BF16)

    if sources == group:
        out_ref[...] = serve(0)
    else:
        span = group * capacity

        def step(i, carry):
            out_ref[pl.ds(pl.multiple_of(i * span, span), span), :] = serve(i * group)
            return carry

        lax.fori_loop(0, sources // group, step, 0)


def own_kernel(shard_rows, scale, len_ref, ids_ref, hot_ref, hot_rows_ref, cot_ref, w_out_ref,
               emb_ref, pick_ref, signal_ref, back_ref):
    tokens = ids_ref.shape[1]
    hot_count = hot_rows_ref.shape[0]
    sources = lax.axis_size("table")
    capacity = tokens // sources
    ids = ids_ref[...]
    table = hot_ref[...]
    high = table_lookup((table // 256).astype(F32).astype(BF16), ids)
    low = table_lookup((table % 256).astype(F32).astype(BF16), ids)
    hot_index = high * 256.0 + low
    cold = hot_index >= hot_count
    row = ids - iota((sources, tokens), 0) * shard_rows
    mark = jnp.where((row >= 0) & (row < shard_rows) & cold, 1.0, 0.0)
    rank = dot_nn(mark.astype(BF16), before_matrix(tokens))
    place = rank + (iota((sources, tokens), 0) * capacity).astype(F32)
    slot = jnp.sum(mark * place, axis=0, keepdims=True) - jnp.where(cold, 0.0, 1.0)
    stacked = jnp.concatenate([slot, hot_index, jnp.zeros((6, tokens), F32)], axis=0)
    columns = jnp.transpose(stacked)
    pick_ref[...] = (
        (iota((tokens, tokens), 1).astype(F32) == columns[:, 0:1]).astype(F32).astype(BF16)
    )
    hot_pick = (iota((tokens, hot_count), 1).astype(F32) == columns[:, 1:2]).astype(F32).astype(BF16)
    emb_ref[...] = dot_nn(hot_pick, hot_rows_ref[...]).astype(BF16)
    users = tokens // MAXLEN
    first_user = (lax.axis_index("table") * lax.axis_size("bal") + lax.axis_index("bal")) * users
    for u in range(users):
        rows = slice(u * MAXLEN, (u + 1) * MAXLEN)
        valid = iota((MAXLEN, 1), 0) < len_ref[first_user + u]
        signal_ref[rows, :] = (jnp.where(valid, cot_ref[rows, :].astype(F32), 0.0) * scale).astype(BF16)
    back_ref[...] = dot_nt(signal_ref[...], w_out_ref[...]).astype(BF16)


def layer_kernel(len_ref, emb_ref, pick_ref, replies_ref, signal_ref, back_ref, w_ref, w_out_ref,
                 out_ref, *rest):
    pieces = rest[:4]
    normed_t, gated_t, grad, gated, slope = rest[4:]
    tokens, features = emb_ref.shape
    head = features // HEADS
    users = tokens // MAXLEN
    bal = lax.axis_size("bal")
    me = lax.axis_index("bal")
    first_user = (lax.axis_index("table") * bal + me) * users
    inv = 1.0 / math.sqrt(head)

    emb = dot_nn(pick_ref[...], replies_ref[...]) + emb_ref[...].astype(F32)
    normed = norm_rows(emb)
    normed_t[...] = jnp.transpose(normed).astype(BF16)
    normed = normed.astype(BF16)

    def part(index):
        hidden = dot_nn(normed, w_ref[:, index * features : (index + 1) * features])
        gate = sigmoid(hidden)
        act = hidden * gate
        slope[:, index * features : (index + 1) * features] = gate * (1.0 + hidden - act)
        return act.astype(BF16)

    gate_part, value_part, query_part, key_part = (part(i) for i in range(4))
    for u in range(users):
        rows = slice(u * MAXLEN, (u + 1) * MAXLEN)
        length = len_ref[first_user + u]
        at = iota((MAXLEN, MAXLEN), 0)
        allowed = (iota((MAXLEN, MAXLEN), 1) <= at) & (at < length)
        weights, slopes, mixes = [], [], []
        for h in range(HEADS):
            cols = slice(h * head, (h + 1) * head)
            score = dot_nt(query_part[rows, cols], key_part[rows, cols]) * inv
            s = sigmoid(score)
            a = score * s
            weight = jnp.where(allowed, a, 0.0).astype(BF16)
            weights.append(weight)
            slopes.append(jnp.where(allowed, s * (1.0 + score - a) * inv, 0.0))
            mixes.append(dot_nn(weight, value_part[rows, cols]))
        mixed = jnp.concatenate(mixes, axis=1)
        centred = mixed - jnp.mean(mixed, axis=-1, keepdims=True)
        rstd = lax.rsqrt(jnp.mean(centred * centred, axis=-1, keepdims=True) + 1e-05)
        unit = centred * rstd
        gate = gate_part[rows].astype(F32)
        gated[rows, :] = (unit * gate).astype(BF16)
        back = back_ref[rows, :].astype(F32)
        d_gate = (back * unit).astype(BF16).astype(F32)
        grad[rows, 0:features] = (d_gate * slope[rows, 0:features]).astype(BF16)
        d_unit = back * gate
        d_mixed = rstd * (
            d_unit
            - jnp.mean(d_unit, axis=-1, keepdims=True)
            - unit * jnp.mean(d_unit * unit, axis=-1, keepdims=True)
        )
        d_mixed = d_mixed.astype(BF16)
        for h in range(HEADS):
            cols = slice(h * head, (h + 1) * head)
            d_mix = d_mixed[:, cols]
            d_weight = dot_nt(d_mix, value_part[rows, cols]).astype(BF16).astype(F32)
            d_score = (d_weight * slopes[h]).astype(BF16)
            d_value = dot_tn(weights[h], d_mix)
            d_query = dot_nn(d_score, key_part[rows, cols])
            d_key = dot_tn(d_score, query_part[rows, cols])
            for index, value in ((1, d_value), (2, d_query), (3, d_key)):
                where = slice(index * features + h * head, index * features + (h + 1) * head)
                grad[rows, where] = (value.astype(BF16).astype(F32) * slope[rows, where]).astype(BF16)
    out_ref[...] = (emb + dot_nn(gated[...], w_out_ref[...])).astype(BF16)
    gated_t[...] = jnp.transpose(gated[...].astype(F32)).astype(BF16)

    block = features // bal
    width = pieces[0].shape[-1]
    total = grad.shape[1]
    low, high = bal // 2, 1
    for r in range(bal):
        start = pl.multiple_of((r ^ me) * block, block)
        left = normed_t[pl.ds(start, block), :]
        first_order, second_order = split_index(r, bal)
        target, index = (pieces[0], pieces[1])[first_order[0]], first_order[1]
        target[index] = dot_nn(left, grad[:, 0:width]).astype(BF16)
        target, index = (pieces[2], pieces[3])[second_order[0]], second_order[1]
        target[index, :, 0 : total - width] = dot_nn(left, grad[:, width:total]).astype(BF16)
        out_left = gated_t[pl.ds(start, block), :]
        target[index, :, total - width : width] = dot_nn(out_left, signal_ref[...]).astype(BF16)


def bit_orders(count):
    bits = [1 << k for k in range(count.bit_length() - 1)]
    half = len(bits) // 2
    return bits, bits[half:] + bits[:half]


def split_index(r, count):
    answers = []
    for order in bit_orders(count):
        bit = order[0]
        same = [k for k in range(count) if (k & bit) == (r & bit)]
        answers.append((0 if r & bit else 1, same.index(r)))
    return answers


def halve(send, keep, order, count):
    members = [k for k in range(count) if not k & order[0]]
    for step, bit in enumerate(order):
        got = lax.ppermute(send, "bal", [(i, i ^ bit) for i in range(count)])
        total = got.astype(F32) + keep.astype(F32)
        if step + 1 == len(order):
            return total[0]
        following = order[step + 1]
        pick = lambda on: [i for i, k in enumerate(members) if bool(k & following) == on]
        send = jnp.stack([total[i] for i in pick(True)]).astype(BF16)
        keep = jnp.stack([total[i] for i in pick(False)])
        members = [k for k in members if not k & following]


def per_device(item_ids, hot_slot, hot_rows, cold_rows, hist_lengths, out_grad, w_uvqk, w_out):
    owners = lax.axis_size("table")
    bal = lax.axis_size("bal")
    tokens = item_ids.shape[0]
    features = hot_rows.shape[1]
    hot_count = hot_rows.shape[0]
    shard_rows = cold_rows.shape[0]
    hidden = w_uvqk.shape[1]
    vmem = pl.BlockSpec(memory_space=pltpu.VMEM)
    smem = pl.BlockSpec(memory_space=pltpu.SMEM)
    hot_table = hot_slot.reshape(-1, LANES)

    everyone = jnp.broadcast_to(item_ids.reshape(1, 1, tokens), (owners, 1, tokens))
    asked = lax.all_to_all(everyone, "table", split_axis=0, concat_axis=0, tiled=True)
    found = pl.pallas_call(
        functools.partial(serve_kernel, hot_count),
        out_shape=jax.ShapeDtypeStruct((tokens, features), BF16),
        in_specs=[vmem] * 3,
        out_specs=vmem,
        compiler_params=pltpu.CompilerParams(vmem_limit_bytes=VM_SERVE),
        name="serve",
    )(asked, hot_table, cold_rows)
    replies = lax.all_to_all(found, "table", split_axis=0, concat_axis=0, tiled=True)

    wide = jax.ShapeDtypeStruct((tokens, features), BF16)
    hot_emb, pick, signal, back = pl.pallas_call(
        functools.partial(own_kernel, shard_rows, 1.0 / math.sqrt(bal * tokens)),
        out_shape=(wide, jax.ShapeDtypeStruct((tokens, tokens), BF16), wide, wide),
        in_specs=[smem] + [vmem] * 5,
        out_specs=(vmem,) * 4,
        compiler_params=pltpu.CompilerParams(vmem_limit_bytes=VM_OWN),
        name="own",
    )(hist_lengths, item_ids.reshape(1, tokens), hot_table, hot_rows, out_grad, w_out)

    width = (hidden + features) // 2
    piece = jax.ShapeDtypeStruct((bal // 2, features // bal, width), BF16)
    layer_out, a_send, a_keep, b_send, b_keep = pl.pallas_call(
        layer_kernel,
        out_shape=(wide,) + (piece,) * 4,
        in_specs=[smem] + [vmem] * 7,
        out_specs=(vmem,) * 5,
        scratch_shapes=[
            pltpu.VMEM((features, tokens), BF16),
            pltpu.VMEM((features, tokens), BF16),
            pltpu.VMEM((tokens, hidden), BF16),
            pltpu.VMEM((tokens, features), BF16),
            pltpu.VMEM((tokens, hidden), F32),
        ],
        compiler_params=pltpu.CompilerParams(vmem_limit_bytes=VM_LAYER),
        name="layer",
    )(hist_lengths, hot_emb, pick, replies, signal, back, w_uvqk, w_out)

    first_order, second_order = bit_orders(bal)
    a = halve(a_send, a_keep, first_order, bal)
    b = halve(b_send, b_keep, second_order, bal)
    grad_first = jnp.concatenate([a, b[:, : hidden - width]], axis=1)
    return (layer_out, grad_first, b[:, hidden - width :])


def solution(mesh):
    return jax.shard_map(
        per_device,
        mesh=mesh,
        in_specs=(
            P(("table", "bal")),
            P(),
            P(),
            P("table", None),
            P(),
            P(("table", "bal"), None),
            P(),
            P(),
        ),
        out_specs=(P(("table", "bal"), None), P(("table", "bal"), None), P(("table", "bal"), None)),
        check_vma=False,
    )
```
